32 devices in a mesh: parts: 1, tm: 32 (over z, y, x, core).
Axes of the slice: x: 2, y: 2, z: 4, core: 2. Of those that a mesh axis runs over, the one named last changes fastest.
Arguments:
- traces: bfloat16 [64, 1151], P(('parts', 'tm')), may hold values from -6 to 6
- templates: bfloat16 [64, 64, 128], P('tm'), may hold values from -0.5 to 0.5
- station_of_slot: int32 [64], replicated, may hold values from 0 to 63, each once
- travel_offsets: int32 [64, 2], replicated, may hold values from 0 to 15
- stack_weights: bfloat16 [2, 128, 64], replicated, may hold values from -6 to 6
Outputs:
- peak_stack: float32 [64, 1024], P('parts', 'tm')
The draws below stay inside these ranges and needn't reach their ends.
Inputs may be any that keep to these rules, and one draw needn't show every extreme that they name: `station_of_slot`: each station stands in exactly one slot. `travel_offsets`: the greatest move-out is reached.
All inputs are finite; a program needn't handle non-finite values.
Results may differ from the reference program's by a relative error of at most 0.0011.
Values may be sent and summed in bfloat16 or wider, within the bound.
A program may use at most 64 MiB of HBM per device.

```python
import jax
import jax.numpy as jnp
from jax import lax

STA_DEV = 2
K = 64
TL = 128
MAXOFF = 16
NB = 2
NPB = 128
S = 64
T_SIZE = 1024
DLEN = 1151
N_TM = 32


def plant(values, own_key, low, top_value):
    place = [jax.random.randint(jax.random.fold_in(own_key, axis), (), 0, length) for axis, length in enumerate(values.shape)]
    longest = values.shape.index(max(values.shape))
    beside = place[:longest] + [(place[longest] + 1) % values.shape[longest]] + place[longest + 1:]
    return values.at[tuple(place)].set(low).at[tuple(beside)].set(top_value)


def block_levels(rng, dims, shards, smallest, largest):
    loudness, own = 1.0, jax.random.fold_in(rng, 6)
    for dim, parts in shards:
        steps = jnp.exp(jax.random.uniform(jax.random.fold_in(own, dim), (parts,), jnp.float32, smallest / len(shards), largest / len(shards)))
        loudness = loudness * jnp.repeat(steps, dims[dim] // parts).reshape([-1 if axis == dim else 1 for axis in range(len(dims))])
    return loudness


def bell_draw(rng, shape, scale, limit, cuts=(), kind=jnp.bfloat16):
    result = jax.random.normal(rng, shape, jnp.float32) * scale
    if len(cuts) > 0:
        result = block_levels(rng, shape, cuts, -0.22, 0.18) * result
    return jnp.clip(result, min=-limit, max=limit).astype(kind)


def setup_inputs(seed: int = 0, part: int = 0) -> dict:
    splits = jax.random.split(jax.random.key(seed), 6)
    part_splits = jax.random.split(jax.random.fold_in(splits[5], part), 6)
    traces = bell_draw(part_splits[0], (S, DLEN), 1.0, 6.0, ((0, 32),))
    templates = bell_draw(splits[1], (S, K, TL), TL ** -0.5, 0.5, ((0, 32),))
    station_of_slot = jax.random.permutation(splits[2], S).astype(jnp.int32)
    travel_offsets = plant(jax.random.randint(splits[3], (S, NB), 0, MAXOFF), jax.random.fold_in(splits[3], 1), 0, MAXOFF - 1).astype(jnp.int32)
    stack_weights = bell_draw(splits[4], (NB, NPB, S), (S // 64) ** -0.5, 6.0)
    return dict(traces=traces, templates=templates, station_of_slot=station_of_slot, travel_offsets=travel_offsets, stack_weights=stack_weights)


def correlate(rows, waveforms):
    row_count = rows.shape[0]
    tmpl_count = waveforms.shape[1]
    tmpl_len = waveforms.shape[2]
    kernel = waveforms.reshape(row_count * tmpl_count, 1, tmpl_len)
    raw_corr = lax.conv_general_dilated(rows[None], kernel, (1,), 'VALID', dimension_numbers=('NCH', 'OIH', 'NCH'), feature_group_count=row_count, preferred_element_type=jnp.float32)[0]
    raw_corr = raw_corr.reshape(row_count, tmpl_count, -1)
    out_len = raw_corr.shape[2]
    squared = rows.astype(jnp.float32)
    squared = squared * squared
    running = jnp.cumsum(jnp.concatenate([jnp.zeros((row_count, 1), jnp.float32), squared], axis=1), axis=1)
    energy = (running[:, tmpl_len:tmpl_len + out_len] - running[:, :out_len]) / tmpl_len
    return (raw_corr / jnp.sqrt(tmpl_len * (energy[:, None, :] + 1e-05))).astype(jnp.bfloat16)

def reference(traces, templates, station_of_slot, travel_offsets, stack_weights):
    grouped = (traces.reshape(N_TM, STA_DEV, DLEN), templates.reshape(N_TM, STA_DEV, K, TL))
    ncc = lax.map(lambda pair: correlate(pair[0], pair[1]), grouped).reshape(S, K, T_SIZE)
    padded = jnp.pad(ncc, ((0, 0), (0, 0), (0, MAXOFF)))
    slot_weights = stack_weights[:, :, station_of_slot]
    slot_offsets = travel_offsets[station_of_slot]

    def one_block(block_id):
        shifted = jax.vmap(lambda row_trace, shift_by: lax.dynamic_slice_in_dim(row_trace, shift_by, T_SIZE, axis=1))(padded, slot_offsets[:, block_id])
        stacked = jnp.dot(slot_weights[block_id], shifted.reshape(S, K * T_SIZE), preferred_element_type=jnp.float32)
        return lax.optimization_barrier(jnp.max(stacked, axis=0))
    peaks = lax.map(one_block, jnp.arange(NB, dtype=jnp.int32))
    return lax.optimization_barrier(jnp.max(peaks, axis=0)).reshape(K, T_SIZE)
```

```python
import functools
import math

import jax
import jax.numpy as jnp
from jax import lax
from jax.experimental import pallas as pl
from jax.experimental.pallas import tpu as pltpu
from jax.sharding import PartitionSpec as P

MESH = pl.DeviceIdType.MESH
LANES = 128


def kernel(
    inner, total, slot_ref, off_ref, tr_ref, tm_ref, st_ref, w_ref, out_ref,
    gtr, gtm, trf, x, r, f, acc, send1, recv1, send2, recv2, local_sem,
):
    outer = gtr.shape[0] + 1
    me = lax.axis_index("tm")
    o, i = me // inner, lax.rem(me, inner)
    rows, data_len = tr_ref.shape
    tmpl, tlen = tm_ref.shape[1:]
    blocks, nodes, stations = w_ref.shape
    slab = r.shape[3]
    span = inner * slab
    lanes = blocks * tmpl
    per_group = LANES // slab

    outer_peers = [lax.rem(o + outer - d, outer) * inner + i for d in range(1, outer)]
    inner_peers = [o * inner + lax.rem(i + d, inner) for d in range(1, inner)]
    barrier = pltpu.get_barrier_semaphore()
    for peer in outer_peers + inner_peers:
        pl.semaphore_signal(barrier, inc=1, device_id={"tm": peer}, device_id_type=MESH)
    pl.semaphore_wait(barrier, outer + inner - 2)

    gathers = []
    for d in range(1, outer):
        for a, (src, dst) in enumerate(((tr_ref, gtr), (tm_ref, gtm))):
            copy = pltpu.make_async_remote_copy(
                src_ref=src, dst_ref=dst.at[d - 1],
                send_sem=send1.at[d - 1, a], recv_sem=recv1.at[d - 1, a],
                device_id={"tm": outer_peers[d - 1]}, device_id_type=MESH,
            )
            copy.start()
            gathers.append(copy)

    trf[...] = jnp.zeros_like(trf)
    one_hot = lax.broadcasted_iota(jnp.int32, (stations, stations), 0) == st_ref[...]
    one_hot = jnp.where(one_hot, 1.0, 0.0).astype(jnp.bfloat16)
    weights = jnp.dot(
        w_ref[...].reshape(blocks * nodes, stations), one_hot, preferred_element_type=jnp.float32
    ).astype(jnp.bfloat16)

    lane = lax.broadcasted_iota(jnp.int32, (LANES, lanes), 1)
    back = LANES - 1 - lax.broadcasted_iota(jnp.int32, (LANES, 1), 0)
    for d in range(outer):
        if d:
            gathers[2 * d - 2].wait()
            gathers[2 * d - 1].wait()
        traces = tr_ref[...] if d == 0 else gtr[d - 1]
        trf[d * rows : (d + 1) * rows, :data_len] = traces.astype(jnp.float32)
        owner = lax.rem(o + d, outer)
        for q in range(rows):
            waveforms = tm_ref[q] if d == 0 else gtm[d - 1, q]
            start = pl.multiple_of(o * span, LANES)
            window = trf[d * rows + q : d * rows + q + 1, pl.ds(start, span + 2 * LANES)]
            station = slot_ref[(owner * inner + i) * rows + q]
            none = jnp.zeros_like(waveforms)
            shifts = [off_ref[station, b] for b in range(blocks)]
            moved = [
                pltpu.roll(jnp.broadcast_to(window, (8, window.shape[1])), lax.rem(window.shape[1] - s, window.shape[1]), 1)[:1]
                for s in shifts
            ]
            for g in range(span // LANES):
                raw, scale = None, None
                for b in range(blocks):
                    piece = moved[b][:, g * LANES : (g + 2) * LANES]
                    piece = jnp.broadcast_to(piece, (LANES, 2 * LANES))
                    hankel = pltpu.roll(piece, LANES + 1, 1, stride=1, stride_axis=0)[:, :tlen]
                    energy = jnp.sum(hankel * hankel, axis=1, keepdims=True) / tlen
                    factor = lax.rsqrt(tlen * (energy + 1e-05))
                    time = o * span + g * LANES + back + shifts[b]
                    factor = jnp.where(time < total, factor, 0.0)
                    side = jnp.concatenate([waveforms if c == b else none for c in range(blocks)], axis=0)
                    part = lax.dot_general(
                        hankel.astype(jnp.bfloat16), side, (((1,), (1,)), ((), ())),
                        preferred_element_type=jnp.float32,
                    )
                    raw = part if raw is None else raw + part
                    factor = jnp.broadcast_to(factor, (LANES, lanes))
                    scale = factor if scale is None else jnp.where(lane < b * tmpl, scale, factor)
                ncc = (raw * scale).astype(jnp.bfloat16)
                x[owner, q, g * per_group : (g + 1) * per_group] = ncc.reshape(per_group, slab, lanes)

    def block_of(index):
        return index // per_group * per_group + per_group - 1 - lax.rem(index, per_group)

    own = pltpu.make_async_copy(x.at[:, :, block_of(i)], r.at[:, i], local_sem)
    own.start()
    sends = []
    for d in range(1, inner):
        copy = pltpu.make_async_remote_copy(
            src_ref=x.at[:, :, block_of(lax.rem(i + d, inner))], dst_ref=r.at[:, i],
            send_sem=send2.at[d - 1], recv_sem=recv2.at[d - 1],
            device_id={"tm": inner_peers[d - 1]}, device_id_type=MESH,
        )
        copy.start()
        sends.append(copy)
    own.wait()
    for copy in sends:
        copy.wait()

    f[...] = r[...].astype(jnp.float32).reshape(stations * slab, lanes)
    for t in range(0, slab, 2):
        pair = [f[pl.ds(t + u, stations, stride=slab), :].astype(jnp.bfloat16) for u in range(2)]
        stacked = jnp.dot(weights, jnp.concatenate(pair, axis=1), preferred_element_type=jnp.float32)
        tops = [
            jnp.max(stacked[b * nodes : (b + 1) * nodes].reshape(nodes // 8, 8, 2 * lanes), axis=0)
            for b in range(blocks)
        ]
        for u in range(2):
            best = tops[0][:, u * lanes : (u + 1) * lanes]
            for b in range(1, blocks):
                best = jnp.where(lane[:8] < b * tmpl, best, tops[b][:, u * lanes : (u + 1) * lanes])
            acc[slab - 1 - t - u : slab - t - u, :] = jnp.max(best, axis=0, keepdims=True)
    peak = acc[...]
    best = peak
    for b in range(1, blocks):
        best = jnp.maximum(best, pltpu.roll(peak, b * tmpl, 1))
    out_ref[...] = best.T[:tmpl]


def on_device(traces, templates, station_of_slot, travel_offsets, stack_weights):
    n = lax.axis_size("tm")
    inner = math.gcd(n, 8)
    outer = n // inner
    rows, data_len = traces.shape
    tmpl, tlen = templates.shape[1:]
    blocks, nodes, stations = stack_weights.shape
    total = data_len - tlen + 1
    slab = total // n
    lanes = blocks * tmpl
    vmem = pl.BlockSpec(memory_space=pltpu.VMEM)
    smem = pl.BlockSpec(memory_space=pltpu.SMEM)
    return pl.pallas_call(
        functools.partial(kernel, inner, total),
        out_shape=jax.ShapeDtypeStruct((tmpl, slab), jnp.float32),
        in_specs=[smem, smem, vmem, vmem, vmem, vmem],
        out_specs=vmem,
        scratch_shapes=[
            pltpu.VMEM((outer - 1, rows, data_len), jnp.bfloat16),
            pltpu.VMEM((outer - 1, rows, tmpl, tlen), jnp.bfloat16),
            pltpu.VMEM((outer * rows, total + 2 * LANES), jnp.float32),
            pltpu.VMEM((outer, rows, inner, slab, lanes), jnp.bfloat16),
            pltpu.VMEM((outer, inner, rows, slab, lanes), jnp.bfloat16),
            pltpu.VMEM((stations * slab, lanes), jnp.float32),
            pltpu.VMEM((slab, lanes), jnp.float32),
            pltpu.SemaphoreType.DMA((outer - 1, 2)),
            pltpu.SemaphoreType.DMA((outer - 1, 2)),
            pltpu.SemaphoreType.DMA((inner - 1,)),
            pltpu.SemaphoreType.DMA((inner - 1,)),
            pltpu.SemaphoreType.DMA,
        ],
        compiler_params=pltpu.CompilerParams(collective_id=0, has_side_effects=True),
    )(station_of_slot, travel_offsets, traces, templates, station_of_slot.reshape(1, stations), stack_weights)


def solution(mesh):
    return jax.shard_map(
        on_device,
        mesh=mesh,
        in_specs=(P(("parts", "tm"), None), P("tm", None, None), P(), P(), P()),
        out_specs=P("parts", "tm"),
        check_vma=False,
    )
```

```python
import functools
import math

import jax
import jax.numpy as jnp
from jax import lax
from jax.experimental import pallas as pl
from jax.experimental.pallas import tpu as pltpu
from jax.sharding import PartitionSpec as P

MESH = pl.DeviceIdType.MESH
LANES = 128


def kernel(
    inner, total, slot_ref, off_ref, tr_ref, tm_ref, st_ref, w_ref, out_ref,
    gtr, gtm, trf, x, r, f, acc, send1, recv1, send2, recv2, local_sem,
):
    outer = gtr.shape[0] + 1
    me = lax.axis_index("tm")
    o, i = me // inner, lax.rem(me, inner)
    rows, data_len = tr_ref.shape
    tmpl, tlen = tm_ref.shape[1:]
    blocks, stations, nodes = w_ref.shape
    slab = r.shape[3]
    span = inner * slab
    lanes = blocks * tmpl
    per_group = LANES // slab

    def across(d):
        if outer & (outer - 1):
            return lax.rem(o + d, outer)
        other = o
        for bit in (1 << k for k in range(outer.bit_length()) if d >> k & 1):
            other = other + bit * (1 - 2 * lax.rem(o // bit, 2))
        return other

    outer_to = [across(d if outer & (outer - 1) == 0 else outer - d) for d in range(1, outer)]
    inner_to = [lax.rem(i + d, inner) for d in range(1, inner)]
    barrier = pltpu.get_barrier_semaphore()
    peers = [z * inner + i for z in outer_to] + [o * inner + k for k in inner_to]
    for peer in peers:
        pl.semaphore_signal(barrier, inc=1, device_id={"tm": peer}, device_id_type=MESH)

    lane = lax.broadcasted_iota(jnp.int32, (LANES, lanes), 1)
    back = LANES - 1 - lax.broadcasted_iota(jnp.int32, (LANES, 1), 0)

    def correlate(d):
        traces = tr_ref[...] if d == 0 else gtr[d - 1]
        trf[d * rows : (d + 1) * rows, :data_len] = traces.astype(jnp.float32)
        owner = across(d)
        for q in range(rows):
            waveforms = tm_ref[q] if d == 0 else gtm[d - 1, q]
            start = pl.multiple_of(o * span, LANES)
            window = trf[d * rows + q : d * rows + q + 1, pl.ds(start, span + 2 * LANES)]
            width = window.shape[1]
            station = slot_ref[(owner * inner + i) * rows + q]
            none = jnp.zeros_like(waveforms)
            shifts = [off_ref[b, station] for b in range(blocks)]
            moved = [
                pltpu.roll(jnp.broadcast_to(window, (8, width)), lax.rem(width - s, width), 1)[:1]
                for s in shifts
            ]
            for g in range(span // LANES):
                raw, scale = None, None
                for b in range(blocks):
                    piece = moved[b][:, g * LANES : (g + 2) * LANES]
                    piece = jnp.broadcast_to(piece, (LANES, 2 * LANES))
                    hankel = pltpu.roll(piece, LANES + 1, 1, stride=1, stride_axis=0)[:, :tlen]
                    energy = jnp.sum(hankel * hankel, axis=1, keepdims=True) / tlen
                    factor = lax.rsqrt(tlen * (energy + 1e-05))
                    time = o * span + g * LANES + back + shifts[b]
                    factor = jnp.where(time < total, factor, 0.0)
                    side = jnp.concatenate([waveforms if c == b else none for c in range(blocks)], axis=0)
                    part = lax.dot_general(
                        hankel.astype(jnp.bfloat16), side, (((1,), (1,)), ((), ())),
                        preferred_element_type=jnp.float32,
                    )
                    raw = part if raw is None else raw + part
                    factor = jnp.broadcast_to(factor, (LANES, lanes))
                    scale = factor if scale is None else jnp.where(lane < b * tmpl, scale, factor)
                ncc = (raw * scale).astype(jnp.bfloat16)
                x[d, q, g * per_group : (g + 1) * per_group] = ncc.reshape(per_group, slab, lanes)

    def block_of(index):
        return index // per_group * per_group + per_group - 1 - lax.rem(index, per_group)

    moves = []

    def exchange(d):
        owner = across(d)
        for k in range(1, inner):
            copy = pltpu.make_async_remote_copy(
                src_ref=x.at[d, :, block_of(inner_to[k - 1])], dst_ref=r.at[owner, i],
                send_sem=send2.at[d, k - 1], recv_sem=recv2.at[d, k - 1],
                device_id={"tm": o * inner + inner_to[k - 1]}, device_id_type=MESH,
            )
            copy.start()
            moves.append(copy)
        own = pltpu.make_async_copy(x.at[d, :, block_of(i)], r.at[owner, i], local_sem.at[d])
        own.start()
        moves.append(own)

    trf[...] = jnp.zeros_like(trf)
    correlate(0)
    pl.semaphore_wait(barrier, outer + inner - 2)

    gathers = []
    for d in range(1, outer):
        for a, (src, dst) in enumerate(((tr_ref, gtr), (tm_ref, gtm))):
            copy = pltpu.make_async_remote_copy(
                src_ref=src, dst_ref=dst.at[d - 1],
                send_sem=send1.at[d - 1, a], recv_sem=recv1.at[d - 1, a],
                device_id={"tm": outer_to[d - 1] * inner + i}, device_id_type=MESH,
            )
            copy.start()
            gathers.append(copy)
    exchange(0)

    one_hot = lax.broadcasted_iota(jnp.int32, (stations, stations), 0) == st_ref[...]
    one_hot = jnp.where(one_hot, 1.0, 0.0).astype(jnp.bfloat16)
    weights = jnp.concatenate([
        lax.dot_general(
            w_ref[b], one_hot, (((0,), (0,)), ((), ())), preferred_element_type=jnp.float32
        ).astype(jnp.bfloat16)
        for b in range(blocks)
    ], axis=0)

    for d in range(1, outer):
        gathers[2 * d - 2].wait_recv()
        gathers[2 * d - 1].wait_recv()
        correlate(d)
        exchange(d)
    for copy in gathers:
        copy.wait_send()
    for copy in moves:
        copy.wait()

    f[...] = r[...].astype(jnp.float32).reshape(stations * slab, lanes)
    for t in range(0, slab, 2):
        pair = [f[pl.ds(t + u, stations, stride=slab), :].astype(jnp.bfloat16) for u in range(2)]
        stacked = jnp.dot(weights, jnp.concatenate(pair, axis=1), preferred_element_type=jnp.float32)
        tops = [
            jnp.max(stacked[b * nodes : (b + 1) * nodes].reshape(nodes // 8, 8, 2 * lanes), axis=0)
            for b in range(blocks)
        ]
        for u in range(2):
            best = tops[0][:, u * lanes : (u + 1) * lanes]
            for b in range(1, blocks):
                best = jnp.where(lane[:8] < b * tmpl, best, tops[b][:, u * lanes : (u + 1) * lanes])
            acc[slab - 1 - t - u : slab - t - u, :] = jnp.max(best, axis=0, keepdims=True)
    peak = acc[...]
    best = peak
    for b in range(1, blocks):
        best = jnp.maximum(best, pltpu.roll(peak, b * tmpl, 1))
    out_ref[...] = best[:, :tmpl]


def on_device(traces, templates, station_of_slot, travel_offsets, stack_weights):
    n = lax.axis_size("tm")
    inner = math.gcd(n, 8)
    outer = n // inner
    rows, data_len = traces.shape
    tmpl, tlen = templates.shape[1:]
    blocks, nodes, stations = stack_weights.shape
    total = data_len - tlen + 1
    slab = total // n
    lanes = blocks * tmpl
    vmem = pl.BlockSpec(memory_space=pltpu.VMEM)
    smem = pl.BlockSpec(memory_space=pltpu.SMEM)
    return pl.pallas_call(
        functools.partial(kernel, inner, total),
        out_shape=jax.ShapeDtypeStruct((slab, tmpl), jnp.float32),
        in_specs=[smem, smem, vmem, vmem, vmem, vmem],
        out_specs=vmem,
        scratch_shapes=[
            pltpu.VMEM((outer - 1, rows, data_len), jnp.bfloat16),
            pltpu.VMEM((outer - 1, rows, tmpl, tlen), jnp.bfloat16),
            pltpu.VMEM((outer * rows, total + 2 * LANES), jnp.float32),
            pltpu.VMEM((outer, rows, inner, slab, lanes), jnp.bfloat16),
            pltpu.VMEM((outer, inner, rows, slab, lanes), jnp.bfloat16),
            pltpu.VMEM((stations * slab, lanes), jnp.float32),
            pltpu.VMEM((slab, lanes), jnp.float32),
            pltpu.SemaphoreType.DMA((outer - 1, 2)),
            pltpu.SemaphoreType.DMA((outer - 1, 2)),
            pltpu.SemaphoreType.DMA((outer, inner - 1)),
            pltpu.SemaphoreType.DMA((outer, inner - 1)),
            pltpu.SemaphoreType.DMA((outer,)),
        ],
        compiler_params=pltpu.CompilerParams(collective_id=0, has_side_effects=True),
    )(
        station_of_slot, travel_offsets.T, traces, templates,
        station_of_slot.reshape(1, stations), stack_weights.swapaxes(1, 2),
    ).T


def solution(mesh):
    return jax.shard_map(
        on_device,
        mesh=mesh,
        in_specs=(P(("parts", "tm"), None), P("tm", None, None), P(), P(), P()),
        out_specs=P("parts", "tm"),
        check_vma=False,
    )
```

```python
import functools
import math

import jax
import jax.numpy as jnp
from jax import lax
from jax.experimental import pallas as pl
from jax.experimental.pallas import tpu as pltpu
from jax.sharding import PartitionSpec as P

MESH = pl.DeviceIdType.MESH
LANES = 128


def kernel(
    inner, total, slot_in, off_in, tr_ref, tm_ref, st_in, w_in, out_ref,
    slot_ref, off_ref, st_ref, w_ref, gtr, gtm, trf, x, r, f, acc,
    load_sem, send1, recv1, send2, recv2, local_sem,
):
    outer = gtr.shape[0]
    me = lax.axis_index("tm")
    o, i = me // inner, lax.rem(me, inner)
    rows, data_len = tr_ref.shape
    tmpl, tlen = tm_ref.shape[1:]
    blocks, stations, nodes = w_in.shape
    slab = r.shape[3]
    span = inner * slab
    lanes = blocks * tmpl
    per_group = LANES // slab

    def origin_of(d):
        if outer & (outer - 1):
            return lax.rem(o + d, outer)
        other = o
        for bit in (1 << k for k in range(outer.bit_length()) if d >> k & 1):
            other = other + bit * (1 - 2 * lax.rem(o // bit, 2))
        return other

    inner_to = [lax.rem(i + d, inner) for d in range(1, inner)]
    barrier = pltpu.get_barrier_semaphore()

    def greet(peer):
        pl.semaphore_signal(barrier, inc=1, device_id={"tm": peer}, device_id_type=MESH)

    for d in range(1, outer):
        greet(origin_of(outer - d if outer & (outer - 1) else d) * inner + i)
    for k in inner_to:
        greet(o * inner + k)

    pairs = (
        (tr_ref, gtr.at[o]), (slot_in, slot_ref), (off_in, off_ref),
        (tm_ref, gtm.at[o]), (st_in, st_ref), (w_in, w_ref),
    )
    loads = [pltpu.make_async_copy(src, dst, load_sem.at[k]) for k, (src, dst) in enumerate(pairs)]
    for copy in loads:
        copy.start()

    lane = lax.broadcasted_iota(jnp.int32, (LANES, lanes), 1)
    back = LANES - 1 - lax.broadcasted_iota(jnp.int32, (LANES, 1), 0)

    def correlate(d):
        owner = origin_of(d)
        trf[d * rows : (d + 1) * rows, :data_len] = gtr[owner].astype(jnp.float32)
        for q in range(rows):
            waveforms = gtm[owner, q]
            start = pl.multiple_of(o * span, LANES)
            window = trf[d * rows + q : d * rows + q + 1, pl.ds(start, span + 2 * LANES)]
            width = window.shape[1]
            station = slot_ref[(owner * inner + i) * rows + q]
            none = jnp.zeros_like(waveforms)
            shifts = [off_ref[b, station] for b in range(blocks)]
            moved = [
                pltpu.roll(jnp.broadcast_to(window, (8, width)), lax.rem(width - s, width), 1)[:1]
                for s in shifts
            ]
            for g in range(span // LANES):
                raw, scale = None, None
                for b in range(blocks):
                    piece = moved[b][:, g * LANES : (g + 2) * LANES]
                    piece = jnp.broadcast_to(piece, (LANES, 2 * LANES))
                    hankel = pltpu.roll(piece, LANES + 1, 1, stride=1, stride_axis=0)[:, :tlen]
                    energy = jnp.sum(hankel * hankel, axis=1, keepdims=True) / tlen
                    factor = lax.rsqrt(tlen * (energy + 1e-05))
                    time = o * span + g * LANES + back + shifts[b]
                    factor = jnp.where(time < total, factor, 0.0)
                    side = jnp.concatenate([waveforms if c == b else none for c in range(blocks)], axis=0)
                    part = lax.dot_general(
                        hankel.astype(jnp.bfloat16), side, (((1,), (1,)), ((), ())),
                        preferred_element_type=jnp.float32,
                    )
                    raw = part if raw is None else raw + part
                    factor = jnp.broadcast_to(factor, (LANES, lanes))
                    scale = factor if scale is None else jnp.where(lane < b * tmpl, scale, factor)
                ncc = (raw * scale).astype(jnp.bfloat16)
                x[d, q, g * per_group : (g + 1) * per_group] = ncc.reshape(per_group, slab, lanes)

    def block_of(index):
        return index // per_group * per_group + per_group - 1 - lax.rem(index, per_group)

    moves = []

    def exchange(d):
        owner = origin_of(d)
        for k in range(1, inner):
            copy = pltpu.make_async_remote_copy(
                src_ref=x.at[d, :, block_of(inner_to[k - 1])], dst_ref=r.at[owner, i],
                send_sem=send2.at[d, k - 1], recv_sem=recv2.at[d, k - 1],
                device_id={"tm": o * inner + inner_to[k - 1]}, device_id_type=MESH,
            )
            copy.start()
            moves.append(copy)
        own = pltpu.make_async_copy(x.at[d, :, block_of(i)], r.at[owner, i], local_sem.at[d])
        own.start()
        moves.append(own)

    def gather(d):
        target = origin_of(outer - d if outer & (outer - 1) else d)
        return [
            pltpu.make_async_remote_copy(
                src_ref=ref.at[o], dst_ref=ref.at[o],
                send_sem=send1.at[d - 1, k], recv_sem=recv1.at[d - 1, k],
                device_id={"tm": target * inner + i}, device_id_type=MESH,
            )
            for k, ref in enumerate((gtr, gtm))
        ]

    trf[...] = jnp.zeros_like(trf)
    for copy in loads:
        copy.wait()
    correlate(0)
    one_hot = lax.broadcasted_iota(jnp.int32, (stations, stations), 0) == st_ref[...]
    one_hot = jnp.where(one_hot, 1.0, 0.0).astype(jnp.bfloat16)
    weights = jnp.concatenate([
        lax.dot_general(
            w_ref[b], one_hot, (((0,), (0,)), ((), ())), preferred_element_type=jnp.float32
        ).astype(jnp.bfloat16)
        for b in range(blocks)
    ], axis=0)
    pl.semaphore_wait(barrier, outer + inner - 2)

    gathers = [copy for d in range(1, outer) for copy in gather(d)]
    for copy in gathers:
        copy.start()
    exchange(0)
    for d in range(1, outer):
        for copy in gathers[2 * d - 2 : 2 * d]:
            copy.wait_recv()
        correlate(d)
        exchange(d)
    for copy in gathers:
        copy.wait_send()
    for copy in moves:
        copy.wait()

    f[...] = r[...].astype(jnp.float32).reshape(stations * slab, lanes)
    for t in range(0, slab, 2):
        pair = [f[pl.ds(t + u, stations, stride=slab), :].astype(jnp.bfloat16) for u in range(2)]
        stacked = jnp.dot(weights, jnp.concatenate(pair, axis=1), preferred_element_type=jnp.float32)
        tops = [
            jnp.max(stacked[b * nodes : (b + 1) * nodes].reshape(nodes // 8, 8, 2 * lanes), axis=0)
            for b in range(blocks)
        ]
        for u in range(2):
            best = tops[0][:, u * lanes : (u + 1) * lanes]
            for b in range(1, blocks):
                best = jnp.where(lane[:8] < b * tmpl, best, tops[b][:, u * lanes : (u + 1) * lanes])
            acc[slab - 1 - t - u : slab - t - u, :] = jnp.max(best, axis=0, keepdims=True)
    peak = acc[...]
    best = peak
    for b in range(1, blocks):
        best = jnp.maximum(best, pltpu.roll(peak, b * tmpl, 1))
    out_ref[...] = best[:, :tmpl]


def on_device(traces, templates, station_of_slot, travel_offsets, stack_weights):
    n = lax.axis_size("tm")
    inner = math.gcd(n, 8)
    outer = n // inner
    rows, data_len = traces.shape
    tmpl, tlen = templates.shape[1:]
    blocks, nodes, stations = stack_weights.shape
    total = data_len - tlen + 1
    slab = total // n
    lanes = blocks * tmpl
    vmem = pl.BlockSpec(memory_space=pltpu.VMEM)
    anywhere = pl.BlockSpec(memory_space=pl.ANY)
    return pl.pallas_call(
        functools.partial(kernel, inner, total),
        out_shape=pltpu.VMEM((slab, tmpl), jnp.float32),
        in_specs=[anywhere] * 6,
        out_specs=vmem,
        scratch_shapes=[
            pltpu.SMEM((stations,), jnp.int32),
            pltpu.SMEM((blocks, stations), jnp.int32),
            pltpu.VMEM((1, stations), jnp.int32),
            pltpu.VMEM((blocks, stations, nodes), jnp.bfloat16),
            pltpu.VMEM((outer, rows, data_len), jnp.bfloat16),
            pltpu.VMEM((outer, rows, tmpl, tlen), jnp.bfloat16),
            pltpu.VMEM((outer * rows, total + 2 * LANES), jnp.float32),
            pltpu.VMEM((outer, rows, inner, slab, lanes), jnp.bfloat16),
            pltpu.VMEM((outer, inner, rows, slab, lanes), jnp.bfloat16),
            pltpu.VMEM((stations * slab, lanes), jnp.float32),
            pltpu.VMEM((slab, lanes), jnp.float32),
            pltpu.SemaphoreType.DMA((6,)),
            pltpu.SemaphoreType.DMA((outer - 1, 2)),
            pltpu.SemaphoreType.DMA((outer - 1, 2)),
            pltpu.SemaphoreType.DMA((outer, inner - 1)),
            pltpu.SemaphoreType.DMA((outer, inner - 1)),
            pltpu.SemaphoreType.DMA((outer,)),
        ],
        compiler_params=pltpu.CompilerParams(collective_id=0, has_side_effects=True),
    )(
        station_of_slot, travel_offsets.T, traces, templates,
        station_of_slot.reshape(1, stations), stack_weights.swapaxes(1, 2),
    ).T


def solution(mesh):
    return jax.shard_map(
        on_device,
        mesh=mesh,
        in_specs=(P(("parts", "tm"), None), P("tm", None, None), P(), P(), P()),
        out_specs=P("parts", "tm"),
        check_vma=False,
    )
```

```python
import functools
import math

import jax
import jax.numpy as jnp
from jax import lax
from jax.experimental import pallas as pl
from jax.experimental.pallas import tpu as pltpu
from jax.sharding import PartitionSpec as P

MESH = pl.DeviceIdType.MESH
LANES = 128


def kernel(
    inner, total, slot_in, off_in, tr_ref, tm_ref, st_in, w_in, out_ref,
    slot_ref, off_ref, st_ref, w_ref, gtr, gtm, trf, x, r, f, acc,
    load_sem, send1, recv1, send2, recv2, local_sem,
):
    outer = gtr.shape[0]
    me = lax.axis_index("tm")
    o, i = me // inner, lax.rem(me, inner)
    rows, data_len = tr_ref.shape
    tmpl, tlen = tm_ref.shape[1:]
    blocks, stations, nodes = w_in.shape
    slab = r.shape[3]
    span = inner * slab
    lanes = blocks * tmpl
    per_group = LANES // slab

    def origin_of(d):
        if outer & (outer - 1):
            return lax.rem(o + d, outer)
        other = o
        for bit in (1 << k for k in range(outer.bit_length()) if d >> k & 1):
            other = other + bit * (1 - 2 * lax.rem(o // bit, 2))
        return other

    inner_to = [lax.rem(i + d, inner) for d in range(1, inner)]
    barrier = pltpu.get_barrier_semaphore()

    def greet(peer):
        pl.semaphore_signal(barrier, inc=1, device_id={"tm": peer}, device_id_type=MESH)

    for d in range(1, outer):
        greet(origin_of(outer - d if outer & (outer - 1) else d) * inner + i)
    for k in inner_to:
        greet(o * inner + k)

    pairs = (
        (tr_ref, gtr.at[o]), (slot_in, slot_ref), (off_in, off_ref),
        (tm_ref, gtm.at[o]), (st_in, st_ref), (w_in, w_ref),
    )
    loads = [pltpu.make_async_copy(src, dst, load_sem.at[k]) for k, (src, dst) in enumerate(pairs)]
    for copy in loads:
        copy.start()

    lane = lax.broadcasted_iota(jnp.int32, (LANES, lanes), 1)
    back = LANES - 1 - lax.broadcasted_iota(jnp.int32, (LANES, 1), 0)

    def correlate(d):
        owner = origin_of(d)
        trf[d * rows : (d + 1) * rows, :data_len] = gtr[owner].astype(jnp.float32)
        for q in range(rows):
            waveforms = gtm[owner, q]
            start = pl.multiple_of(o * span, LANES)
            window = trf[d * rows + q : d * rows + q + 1, pl.ds(start, span + 2 * LANES)]
            width = window.shape[1]
            station = slot_ref[(owner * inner + i) * rows + q]
            none = jnp.zeros_like(waveforms)
            shifts = [off_ref[b, station] for b in range(blocks)]
            moved = [
                pltpu.roll(jnp.broadcast_to(window, (8, width)), lax.rem(width - s, width), 1)[:1]
                for s in shifts
            ]
            for g in range(span // LANES):
                raw, scale = None, None
                for b in range(blocks):
                    piece = moved[b][:, g * LANES : (g + 2) * LANES]
                    piece = jnp.broadcast_to(piece, (LANES, 2 * LANES))
                    hankel = pltpu.roll(piece, LANES + 1, 1, stride=1, stride_axis=0)[:, :tlen]
                    energy = jnp.sum(hankel * hankel, axis=1, keepdims=True) / tlen
                    factor = lax.rsqrt(tlen * (energy + 1e-05))
                    time = o * span + g * LANES + back + shifts[b]
                    factor = jnp.where(time < total, factor, 0.0)
                    side = jnp.concatenate([waveforms if c == b else none for c in range(blocks)], axis=0)
                    part = lax.dot_general(
                        hankel.astype(jnp.bfloat16), side, (((1,), (1,)), ((), ())),
                        preferred_element_type=jnp.float32,
                    )
                    raw = part if raw is None else raw + part
                    factor = jnp.broadcast_to(factor, (LANES, lanes))
                    scale = factor if scale is None else jnp.where(lane < b * tmpl, scale, factor)
                ncc = (raw * scale).astype(jnp.bfloat16)
                x[d, g * per_group : (g + 1) * per_group, q] = ncc.reshape(per_group, slab, lanes)

    def block_of(index):
        return index // per_group * per_group + per_group - 1 - lax.rem(index, per_group)

    moves = []

    def exchange(d):
        owner = origin_of(d)
        for k in range(1, inner):
            copy = pltpu.make_async_remote_copy(
                src_ref=x.at[d, block_of(inner_to[k - 1])], dst_ref=r.at[owner, i],
                send_sem=send2.at[d, k - 1], recv_sem=recv2.at[d, k - 1],
                device_id={"tm": o * inner + inner_to[k - 1]}, device_id_type=MESH,
            )
            copy.start()
            moves.append(copy)
        own = pltpu.make_async_copy(x.at[d, block_of(i)], r.at[owner, i], local_sem.at[d])
        own.start()
        moves.append(own)

    def gather(d):
        target = origin_of(outer - d if outer & (outer - 1) else d)
        return [
            pltpu.make_async_remote_copy(
                src_ref=ref.at[o], dst_ref=ref.at[o],
                send_sem=send1.at[d - 1, k], recv_sem=recv1.at[d - 1, k],
                device_id={"tm": target * inner + i}, device_id_type=MESH,
            )
            for k, ref in enumerate((gtr, gtm))
        ]

    trf[...] = jnp.zeros_like(trf)
    for copy in loads:
        copy.wait()
    correlate(0)
    one_hot = lax.broadcasted_iota(jnp.int32, (stations, stations), 0) == st_ref[...]
    one_hot = jnp.where(one_hot, 1.0, 0.0).astype(jnp.bfloat16)
    weights = jnp.concatenate([
        lax.dot_general(
            w_ref[b], one_hot, (((0,), (0,)), ((), ())), preferred_element_type=jnp.float32
        ).astype(jnp.bfloat16)
        for b in range(blocks)
    ], axis=0)
    pl.semaphore_wait(barrier, outer + inner - 2)

    gathers = [copy for d in range(1, outer) for copy in gather(d)]
    for copy in gathers:
        copy.start()
    exchange(0)
    for d in range(1, outer):
        for copy in gathers[2 * d - 2 : 2 * d]:
            copy.wait_recv()
        correlate(d)
        exchange(d)
    for d in range(outer):
        for copy in moves[d * inner : (d + 1) * inner - 1]:
            copy.wait_recv()
        moves[(d + 1) * inner - 1].wait()
        owner = origin_of(d)
        part = inner * rows * slab
        at = pl.multiple_of(owner * part, part)
        f[pl.ds(at, part), :] = r[owner].astype(jnp.float32).reshape(part, lanes)
    half = lax.broadcasted_iota(jnp.int32, (stations, lanes), 1) < tmpl
    for t in range(0, slab, 4):
        line = [f[pl.ds(t + u, stations, stride=slab), :] for u in range(4)]
        turn = [pltpu.roll(v, tmpl, 1) for v in line]
        best = None
        for b in range(blocks):
            low, high = (line, turn) if b == 0 else (turn, line)
            rhs = jnp.concatenate(
                [jnp.where(half, low[u], high[u + 1]).astype(jnp.bfloat16) for u in (0, 2)], axis=1
            )
            stacked = jnp.dot(
                weights[b * nodes : (b + 1) * nodes], rhs, preferred_element_type=jnp.float32
            )
            top = jnp.max(stacked.reshape(nodes // 8, 8, 2 * lanes), axis=0)
            best = top if best is None else jnp.maximum(best, top)
        best = jnp.max(best, axis=0, keepdims=True)
        for u in range(4):
            acc[slab - 1 - t - u : slab - t - u, :tmpl] = best[:, u * tmpl : (u + 1) * tmpl]
    out_ref[...] = acc[:, :tmpl]
    for copy in gathers:
        copy.wait_send()
    for d in range(outer):
        for copy in moves[d * inner : (d + 1) * inner - 1]:
            copy.wait_send()


def on_device(traces, templates, station_of_slot, travel_offsets, stack_weights):
    n = lax.axis_size("tm")
    inner = math.gcd(n, 8)
    outer = n // inner
    rows, data_len = traces.shape
    tmpl, tlen = templates.shape[1:]
    blocks, nodes, stations = stack_weights.shape
    total = data_len - tlen + 1
    slab = total // n
    lanes = blocks * tmpl
    vmem = pl.BlockSpec(memory_space=pltpu.VMEM)
    anywhere = pl.BlockSpec(memory_space=pl.ANY)
    return pl.pallas_call(
        functools.partial(kernel, inner, total),
        out_shape=pltpu.VMEM((slab, tmpl), jnp.float32),
        in_specs=[anywhere] * 6,
        out_specs=vmem,
        scratch_shapes=[
            pltpu.SMEM((stations,), jnp.int32),
            pltpu.SMEM((blocks, stations), jnp.int32),
            pltpu.VMEM((1, stations), jnp.int32),
            pltpu.VMEM((blocks, stations, nodes), jnp.bfloat16),
            pltpu.VMEM((outer, rows, data_len), jnp.bfloat16),
            pltpu.VMEM((outer, rows, tmpl, tlen), jnp.bfloat16),
            pltpu.VMEM((outer * rows, total + 2 * LANES), jnp.float32),
            pltpu.VMEM((outer, inner, rows, slab, lanes), jnp.bfloat16),
            pltpu.VMEM((outer, inner, rows, slab, lanes), jnp.bfloat16),
            pltpu.VMEM((stations * slab, lanes), jnp.float32),
            pltpu.VMEM((slab, lanes), jnp.float32),
            pltpu.SemaphoreType.DMA((6,)),
            pltpu.SemaphoreType.DMA((outer - 1, 2)),
            pltpu.SemaphoreType.DMA((outer - 1, 2)),
            pltpu.SemaphoreType.DMA((outer, inner - 1)),
            pltpu.SemaphoreType.DMA((outer, inner - 1)),
            pltpu.SemaphoreType.DMA((outer,)),
        ],
        compiler_params=pltpu.CompilerParams(collective_id=0, has_side_effects=True),
    )(
        station_of_slot, travel_offsets.T, traces, templates,
        station_of_slot.reshape(1, stations), stack_weights.swapaxes(1, 2),
    ).T


def solution(mesh):
    return jax.shard_map(
        on_device,
        mesh=mesh,
        in_specs=(P(("parts", "tm"), None), P("tm", None, None), P(), P(), P()),
        out_specs=P("parts", "tm"),
        check_vma=False,
    )
```
